256 devices in a mesh: frame: 32 (over z_lo, y, core), row: 8 (over x, z_hi).
Axes of the slice: x: 4, y: 4, z: 8 (z_hi: 2, z_lo: 4; z = z_hi * 4 + z_lo), core: 2. Of those that a mesh axis runs over, the one named last changes fastest.
Arguments:
- spatial_q: bfloat16 [32, 1024, 3072], P('frame', 'row'), may hold values from -6 to 6
- spatial_k: bfloat16 [32, 1024, 3072], P('frame', 'row'), may hold values from -6 to 6
- spatial_v: bfloat16 [32, 1024, 3072], P('frame', 'row'), may hold values from -6 to 6
- norm_gain: float32 [3072], replicated, may hold values from 0.5 to 1.5
- temporal_weight: bfloat16 [3072, 3, 3072], P(None, None, 'row'), may hold values from -0.625 to 0.625
Outputs:
- temporal_out: bfloat16 [32, 1024, 3072], P('frame', 'row')
The draws below stay inside these ranges and needn't reach their ends.
All inputs are finite; a program needn't handle non-finite values.
Results may differ from the reference program's by a relative error of at most 0.0083.
Values may be sent and summed in bfloat16 or wider, within the bound.
A program may use at most 64 MiB of HBM per device.

```python
from functools import partial
import jax
import jax.numpy as jnp
from jax import lax

D = 3072
HEADS = 24
AGENTS = 128
TOK_DEV = 128
FRAMES = 32
TOK_FRAME = 1024


def spatial_pair(key):
    shape = (FRAMES, TOK_FRAME, D)
    subkeys = jax.random.split(jax.random.fold_in(key, 71), 2)
    queries = jnp.clip(jax.random.normal(subkeys[0], shape, jnp.float32), -5.9, 5.9)
    keys_out = jnp.clip(jax.random.normal(subkeys[1], shape, jnp.float32), -5.9, 5.9)
    return (queries.astype(jnp.bfloat16), keys_out.astype(jnp.bfloat16))


def draw_spatial_q(key, part):
    return spatial_pair(key)[0]


def draw_spatial_k(key, part):
    return spatial_pair(key)[1]


def draw_temporal_weight(key, part):
    subkeys = jax.random.split(jax.random.fold_in(key, 53), 1)
    base = jax.random.normal(subkeys[0], (D, 3, D), jnp.float32) / jnp.sqrt(jnp.float32(D))
    return jnp.clip(base, -0.625, 0.625).astype(jnp.bfloat16)


def block_scale(own_key, extent, pieces, smallest, top_value):
    def one(axis_at, shards_of):
        heights = jax.random.uniform(jax.random.fold_in(jax.random.fold_in(own_key, 6), axis_at), (shards_of,), jnp.float32, smallest / len(pieces), top_value / len(pieces))
        return jnp.repeat(jnp.exp(heights), extent[axis_at] // shards_of).reshape((-1,) + (1,) * (len(extent) - axis_at - 1))

    loudness = one(*pieces[0])
    for cut in pieces[1:]:
        loudness = loudness * one(*cut)
    return loudness


def noise(rng, extent, deviation, limit, cuts=(), held_as=jnp.bfloat16):
    drawn = deviation * jax.random.normal(rng, extent, jnp.float32)
    if cuts:
        drawn = drawn * block_scale(rng, extent, cuts, -0.22, 0.18)
    return jnp.clip(drawn, -limit, limit).astype(held_as)


def setup_inputs(seed: int = 0) -> dict:
    arg_keys = jax.random.split(jax.random.key(seed), 6)
    spatial_q = draw_spatial_q(jax.random.fold_in(arg_keys[5], 71), 0)
    spatial_k = draw_spatial_k(jax.random.fold_in(arg_keys[5], 71), 0)
    spatial_v = noise(arg_keys[2], (FRAMES, TOK_FRAME, D), 1.0, 6.0, ((0, 32), (1, 8)))
    norm_gain = jnp.clip(1.0 + 0.1 * jax.random.normal(arg_keys[3], (D,), jnp.float32), 0.5, 1.5)
    temporal_weight = draw_temporal_weight(jax.random.fold_in(arg_keys[5], 71), 0)
    return {"spatial_q": spatial_q, "spatial_k": spatial_k, "spatial_v": spatial_v, "norm_gain": norm_gain, "temporal_weight": temporal_weight}


epsilon = 1e-06

def rounded(values):
    return lax.optimization_barrier(values.astype(jnp.bfloat16)).astype(jnp.float32)

def spatial_frame(gain, operands):
    queries, keys_in, values_in = operands
    head_size = D // HEADS
    scale = head_size ** (-0.5)
    pool_size = TOK_FRAME // AGENTS
    agents = lax.optimization_barrier(jnp.mean(queries.reshape(AGENTS, pool_size, D), axis=1, dtype=jnp.float32)).astype(jnp.bfloat16)
    query_heads = queries.astype(jnp.float32).reshape(TOK_FRAME, HEADS, head_size)
    key_heads = keys_in.astype(jnp.float32).reshape(TOK_FRAME, HEADS, head_size)
    value_heads = values_in.astype(jnp.float32).reshape(TOK_FRAME, HEADS, head_size)
    agent_heads = agents.astype(jnp.float32).reshape(AGENTS, HEADS, head_size)
    agent_scores = jnp.einsum('ahd,thd->hat', agent_heads, key_heads) * scale
    peak = lax.optimization_barrier(jnp.max(agent_scores, axis=-1, keepdims=True))
    agent_weights = jnp.exp(agent_scores - peak)
    agent_totals = lax.optimization_barrier(jnp.sum(agent_weights, axis=-1))
    agent_numer = jnp.einsum('hat,thd->had', rounded(agent_weights), value_heads)
    agent_values = rounded(agent_numer / agent_totals[:, :, None])
    token_scores = jnp.einsum('thd,ahd->hta', query_heads, agent_heads) * scale
    token_weights = rounded(jax.nn.softmax(token_scores, axis=-1))
    spatial_out = jnp.einsum('hta,had->thd', token_weights, agent_values).reshape(TOK_FRAME, D)
    mean_square = lax.optimization_barrier(jnp.mean(spatial_out * spatial_out, axis=-1, keepdims=True))
    return (spatial_out * lax.rsqrt(mean_square + epsilon) * gain).astype(jnp.bfloat16)

def temporal_block(weight_matrix, block):
    head_size = D // HEADS
    scale = head_size ** (-0.5)
    locations = block.shape[1]
    projected = jnp.dot(block.reshape(-1, D), weight_matrix, preferred_element_type=jnp.float32)
    qkv = rounded(projected).reshape(FRAMES, locations, 3, HEADS, head_size)
    scores = jnp.einsum('flhd,glhd->lhfg', qkv[:, :, 0], qkv[:, :, 1]) * scale
    weights = rounded(jax.nn.softmax(scores, axis=-1))
    result = jnp.einsum('lhfg,glhd->flhd', weights, qkv[:, :, 2])
    return result.reshape(FRAMES, locations, D).astype(jnp.bfloat16)

def reference(spatial_q, spatial_k, spatial_v, norm_gain, temporal_weight):
    normed = lax.map(partial(spatial_frame, norm_gain), (spatial_q, spatial_k, spatial_v))
    block_count = TOK_FRAME // TOK_DEV
    blocks = normed.reshape(FRAMES, block_count, TOK_DEV, D).transpose(1, 0, 2, 3)
    outputs = lax.map(partial(temporal_block, temporal_weight.reshape(D, 3 * D)), blocks)
    return outputs.transpose(1, 0, 2, 3).reshape(FRAMES, TOK_FRAME, D)
```

```python
import jax
import jax.numpy as jnp
from jax import lax
from jax.experimental import pallas as pl
from jax.experimental.pallas import tpu as pltpu
from jax.sharding import PartitionSpec as P

D = 3072
HEAD = 128
TOK = 128
XCOLS = D // 4
XHEADS = XCOLS // HEAD
HALF_TOK = 4 * TOK
LOC = 16
NCOLS = D // 8
NHEADS = NCOLS // HEAD
SCALE = HEAD ** (-0.5)
EPS = 1e-06
F32 = jnp.float32
BF16 = jnp.bfloat16
MESH = pl.DeviceIdType.MESH


def aligned(i, n):
    return pl.multiple_of(i * n, n)


def kernel(
    q_hbm, k_hbm, v_hbm, gain, w_hbm, out,
    qx, kx, vx, ag, tw, pb, nb, st, sb, wv, ws, xb, acc, ssq, of, ob, rb,
    a_send, a_recv, a_loc, z_send, z_recv, w_loc, w1_send, w1_recv, w2_send, w2_recv,
    b_send, b_recv, b_loc, x_send, x_recv, s_send, s_recv, c_send, c_recv, c_loc, o_send, o_recv, o_loc,
):
    f = lax.axis_index("frame")
    r = lax.axis_index("row")
    zl, y, c = f // 8, (f // 2) % 4, f % 2
    x, zh = r // 2, r % 2

    def dev(zl_, y_, c_, x_, zh_):
        return ((zl_ * 4 + y_) * 2 + c_, x_ * 2 + zh_)

    def remote(src, dst, ss, rs, to):
        return pltpu.make_async_remote_copy(src, dst, ss, rs, device_id=to, device_id_type=MESH)

    z_dev = dev(zl, y, c, x, 1 - zh)
    sib = dev(zl, y, 1 - c, x, zh)
    owner = c == zh

    def a_copy(t, dx):
        src, dst = ((q_hbm, qx), (k_hbm, kx), (v_hbm, vx))[t]
        xp = (x + dx) % 4
        return remote(
            src.at[:, pl.ds(aligned(xp, XCOLS), XCOLS)],
            dst.at[pl.ds(aligned(x, TOK), TOK), :],
            a_send.at[t, dx], a_recv.at[t, dx], dev(zl, y, c, xp, zh),
        )

    def a_local(t):
        src, dst = ((q_hbm, qx), (k_hbm, kx), (v_hbm, vx))[t]
        return pltpu.make_async_copy(
            src.at[:, pl.ds(aligned(x, XCOLS), XCOLS)], dst.at[pl.ds(aligned(x, TOK), TOK), :], a_loc.at[t]
        )

    def a_wait(t):
        for dx in (1, 3, 2):
            a_copy(t, dx).wait_recv()
        a_local(t).wait()

    for t in range(3):
        for dx in (1, 3, 2):
            a_copy(t, dx).start()
        a_local(t).start()

    rows_y = pl.ds(aligned(y, 768), 768)

    def w1_copy(i):
        return remote(w_hbm.at[i, rows_y, :], wv.at[i, rows_y, :], w1_send.at[i], w1_recv.at[i], z_dev)

    def w_local():
        return pltpu.make_async_copy(w_hbm, wv, w_loc)

    def w2_copy(i, dy):
        to = dev(zl, (y + dy) % 4, c, x, zh)
        return remote(wv.at[i, rows_y, :], wv.at[i, rows_y, :], w2_send.at[i, dy], w2_recv.at[i, dy], to)

    @pl.when(owner)
    def _():
        for i in range(3):
            w1_copy(i).start()
        w_local().start()

    def w_forward(i):
        @pl.when(jnp.logical_not(owner))
        def _():
            w1_copy(i).wait_recv()
            for dy in (1, 3, 2):
                w2_copy(i, dy).start()

    a_wait(0)
    pool = (
        lax.broadcasted_iota(jnp.int32, (64, HALF_TOK), 1) // 8 == lax.broadcasted_iota(jnp.int32, (64, HALF_TOK), 0)
    ).astype(F32) * 0.125
    ag[zh] = jnp.dot(pool.astype(BF16), qx[...], preferred_element_type=F32).astype(BF16)
    ag_copy = remote(ag.at[zh], ag.at[zh], z_send.at[0], z_recv.at[0], z_dev)
    ag_copy.start()
    ag_copy.wait_recv()

    def nt(a, b):
        return lax.dot_general(a, b, (((1,), (1,)), ((), ())), preferred_element_type=F32)

    def head(h):
        return slice(h * HEAD, (h + 1) * HEAD)

    def agents(h):
        return ag[:, :, head(h)].reshape(2 * 64, HEAD)

    for h in range(XHEADS):
        s = nt(qx[:, head(h)], agents(h)) * SCALE
        e = jnp.exp(s - jnp.max(s, axis=1, keepdims=True))
        tw[h] = e * (1.0 / jnp.sum(e, axis=1, keepdims=True))
    w_forward(0)

    a_wait(1)
    lane = lax.broadcasted_iota(jnp.int32, (128, 128), 1)
    stats = jnp.where(lane < 8, 0.0, 1.0)
    for h in range(XHEADS):
        s = nt(agents(h), kx[:, head(h)]) * SCALE
        m = jnp.max(s, axis=1, keepdims=True)
        e = jnp.exp(s - m)
        pb[h] = e.astype(BF16)
        stats = jnp.where(lane == h, m, stats)
        stats = jnp.where(lane == 8 + h, jnp.sum(e, axis=1, keepdims=True), stats)
    st[zh] = stats.T[0:16, :]
    st_copy = remote(st.at[zh], st.at[zh], z_send.at[1], z_recv.at[1], z_dev)
    st_copy.start()
    w_forward(1)
    a_wait(2)
    for h in range(XHEADS):
        nb[zh, h] = jnp.dot(pb[h], vx[:, head(h)], preferred_element_type=F32).astype(BF16)
    nb_copy = remote(nb.at[zh], nb.at[zh], z_send.at[2], z_recv.at[2], z_dev)
    nb_copy.start()
    st_copy.wait_recv()
    m0, m1 = st[0, 0:8, :], st[1, 0:8, :]
    l0, l1 = st[0, 8:16, :], st[1, 8:16, :]
    peak = jnp.maximum(m0, m1)
    e0, e1 = jnp.exp(m0 - peak), jnp.exp(m1 - peak)
    inv = 1.0 / (l0 * e0 + l1 * e1)
    s0, s1 = e0 * inv, e1 * inv
    nb_copy.wait_recv()

    for h in range(XHEADS):
        t = tw[h]
        both = jnp.concatenate([(t * s0[h : h + 1, :]).astype(BF16), (t * s1[h : h + 1, :]).astype(BF16)], axis=1)
        sb[:, head(h)] = jnp.dot(
            both, nb[:, h].reshape(256, HEAD), preferred_element_type=F32
        ).astype(BF16)

    me = (zl * 4 + y) * 2 + zh

    def b_copy(d):
        zl_, y_, zh_ = (zl + d // 8) % 4, (y + (d // 2) % 4) % 4, (zh + d % 2) % 2
        g = y_ * 8 + zh_ * 4 + zl_
        return remote(
            sb.at[pl.ds(aligned(g, LOC), LOC), :],
            xb.at[c, x, pl.ds(aligned(me, LOC), LOC), :],
            b_send.at[d], b_recv.at[d], dev(zl_, y_, c, x, zh_),
        )

    def b_wait(d):
        zl_, y_, zh_ = (zl + 4 - d // 8) % 4, (y + 4 - (d // 2) % 4) % 4, (zh + d % 2) % 2
        row = (zl_ * 4 + y_) * 2 + zh_
        dst = xb.at[c, x, pl.ds(aligned(row, LOC), LOC), :]
        remote(dst, dst, b_send.at[d], b_recv.at[d], z_dev).wait_recv()

    group = y * 8 + zh * 4 + zl
    own = pltpu.make_async_copy(
        sb.at[pl.ds(aligned(group, LOC), LOC), :], xb.at[c, x, pl.ds(aligned(me, LOC), LOC), :], b_loc
    )
    own.start()

    @pl.loop(1, 32)
    def _(d):
        b_copy(d).start()

    w_forward(2)

    @pl.when(owner)
    def _():
        w_local().wait()

    @pl.when(jnp.logical_not(owner))
    def _():
        for i in range(3):
            for dy in (1, 3, 2):
                dst = wv.at[i, pl.ds(aligned((y + 4 - dy) % 4, 768), 768), :]
                remote(dst, dst, w2_send.at[i, dy], w2_recv.at[i, dy], z_dev).wait_recv()
            for dy in (1, 3, 2):
                w2_copy(i, dy).wait_send()

    @pl.loop(0, D // 128)
    def _(kc):
        g = jnp.broadcast_to(gain[pl.ds(kc, 1), :], (128, 128)).T
        rows = pl.ds(aligned(kc, 128), 128)
        for i in range(3):
            for j in range(NHEADS):
                piece = wv[i, rows, head(j)].astype(F32) * g
                ws[rows, i * NCOLS + j * HEAD : i * NCOLS + (j + 1) * HEAD] = piece.astype(BF16)

    left, right, far = (x + 3) % 4, (x + 1) % 4, (x + 2) % 4

    def block(half, col, s, lo=0, n=128):
        zl_ = (zl + 4 - s) % 4
        return xb.at[half, col, pl.ds(pl.multiple_of(zl_ * 128 + lo, 64), n), :]

    def x_own(s, i):
        b = block(c, x, s)
        return remote(b, b, x_send.at[s, i], x_recv.at[s, i], dev(zl, y, c, (right, left)[i], zh))

    def x_fwd(s, i):
        b = block(c, (left, right)[i], s, 64 * i, 64)
        return remote(b, b, x_send.at[s, 2 + i], x_recv.at[s, 2 + i], dev(zl, y, c, (right, left)[i], zh))

    def x_got(s, i):
        col = (left, right, far, far)[i]
        b = block(c, col, s, *((0, 128), (0, 128), (0, 64), (64, 64))[i])
        return remote(b, b, x_send.at[s, i], x_recv.at[s, i], z_dev)

    def to_sib(s, i):
        b = block(c, (x, left, right, far)[i], s)
        return remote(b, b, s_send.at[s, i], s_recv.at[s, i], sib)

    def from_sib(s, i):
        b = block(1 - c, (x, left, right, far)[i], s)
        return remote(b, b, s_send.at[s, i], s_recv.at[s, i], sib)

    def mm(half, col, first=False):
        rows_w = pl.ds(aligned(col, XCOLS), XCOLS)

        @pl.loop(0, 2)
        def _(i):
            src = xb[half, col, pl.ds(aligned(i, 256), 256), :]
            rows = pl.ds(pl.multiple_of(half * 512 + i * 256, 256), 256)
            p = jnp.dot(src, ws[rows_w, :], preferred_element_type=F32)
            wide = src.astype(F32)
            sq = jnp.broadcast_to(jnp.sum(wide * wide, axis=1, keepdims=True), (256, 128))
            for j in range(3 * NHEADS):
                if first:
                    acc[j, rows, :] = p[:, head(j)]
                else:
                    acc[j, rows, :] += p[:, head(j)]
            if first:
                ssq[rows, :] = sq
            else:
                ssq[rows, :] += sq

    for s in range(6):
        if s < 4:
            if s == 0:
                own.wait()
            for d in range(8 * s, 8 * s + 8):
                if d:
                    b_wait(d)
            x_own(s, 0).start()
            x_own(s, 1).start()
            to_sib(s, 0).start()
        if 1 <= s < 5:
            for i in range(2):
                x_got(s - 1, i).wait_recv()
                x_fwd(s - 1, i).start()
                to_sib(s - 1, 1 + i).start()
        if s == 3:
            mm(c, x, True)
        if s == 4:
            for q in range(4):
                from_sib(q, 0).wait_recv()
            mm(1 - c, x, True)
        if s >= 2:
            for i in (2, 3):
                x_got(s - 2, i).wait_recv()
            to_sib(s - 2, 3).start()
        if s == 4:
            mm(c, left)
            mm(c, right)
    for q in range(4):
        from_sib(q, 1).wait_recv()
        from_sib(q, 2).wait_recv()
    mm(1 - c, left)
    mm(1 - c, right)
    mm(c, far)
    for q in range(4):
        from_sib(q, 3).wait_recv()
    mm(1 - c, far)
    ssq[...] = lax.rsqrt(ssq[...] * (1.0 / D) + EPS)

    same = (
        lax.broadcasted_iota(jnp.int32, (128, 128), 0) // 32 == lax.broadcasted_iota(jnp.int32, (128, 128), 1) // 32
    )

    def c_copy(d, h):
        zl_, y_, c_ = (zl + d // 8) % 4, (y + (d // 2) % 4) % 4, (c + d % 2) % 2
        row = c_ * 512 + (zl_ * 4 + y_) * 32 + h * LOC
        hs = (h + 2 - zh) % 2
        return remote(
            ob.at[pl.ds(pl.multiple_of(row, LOC), LOC), :],
            rb.at[pl.ds(aligned(group, LOC), LOC), pl.ds(aligned(c, NCOLS), NCOLS)],
            c_send.at[hs, d], c_recv.at[hs, d], dev(zl_, y_, c_, x, h),
        )

    def c_own():
        row = c * 512 + (zl * 4 + y) * 32 + zh * LOC
        return pltpu.make_async_copy(
            ob.at[pl.ds(pl.multiple_of(row, LOC), LOC), :],
            rb.at[pl.ds(aligned(group, LOC), LOC), pl.ds(aligned(c, NCOLS), NCOLS)], c_loc,
        )

    for part in range(2):

        @pl.loop(part * 4, part * 4 + 4)
        def _(b):
            picks = [pl.ds(b * 4 + i, 32, stride=32) for i in range(4)]
            norm = jnp.concatenate([ssq[p, :] for p in picks], axis=0)

            def rows_of(j):
                return (jnp.concatenate([acc[j, p, :] for p in picks], axis=0) * norm).astype(BF16)

            for h in range(NHEADS):
                s = nt(rows_of(h), rows_of(NHEADS + h)) * SCALE
                s = jnp.where(same, s, -1e30)
                e = jnp.exp(s - jnp.max(s, axis=1, keepdims=True))
                p = (e * (1.0 / jnp.sum(e, axis=1, keepdims=True))).astype(BF16)
                o = jnp.dot(p, rows_of(2 * NHEADS + h), preferred_element_type=F32)
                for i in range(4):
                    of[h, picks[i], :] = o[32 * i : 32 * i + 32, :]

        @pl.loop(0, 32)
        def _(k):
            rows = pl.ds(pl.multiple_of(k * 32 + part * LOC, LOC), LOC)
            for h in range(NHEADS):
                ob[rows, head(h)] = of[h, rows, :].astype(BF16)

        @pl.loop(1, 32)
        def _(d):
            c_copy(d, part).start()

        @pl.when(zh == part)
        def _():
            c_own().start()

        @pl.when(zh != part)
        def _():
            c_copy(0, part).start()

    c_own().wait()

    def c_wait(hs, d):
        zl_, y_, c_ = (zl + 4 - d // 8) % 4, (y + 4 - (d // 2) % 4) % 4, (c + d % 2) % 2
        zh_ = (zh + hs) % 2
        g = y_ * 8 + zh_ * 4 + zl_
        dst = rb.at[pl.ds(aligned(g, LOC), LOC), pl.ds(aligned(c_, NCOLS), NCOLS)]
        remote(dst, dst, c_send.at[hs, d], c_recv.at[hs, d], z_dev).wait_recv()

    @pl.loop(1, 64)
    def _(d):
        c_wait(d // 32, d % 32)

    def o_copy(dx):
        xp = (x + dx) % 4
        return remote(
            rb.at[pl.ds(aligned(xp, TOK), TOK), :], out.at[:, pl.ds(aligned(x, XCOLS), XCOLS)],
            o_send.at[dx], o_recv.at[dx], dev(zl, y, c, xp, zh),
        )

    for dx in (1, 3, 2):
        o_copy(dx).start()
    mine = pltpu.make_async_copy(
        rb.at[pl.ds(aligned(x, TOK), TOK), :], out.at[:, pl.ds(aligned(x, XCOLS), XCOLS)], o_loc
    )
    mine.start()

    for t in range(3):
        for dx in (1, 3, 2):
            a_copy(t, dx).wait_send()

    @pl.when(owner)
    def _():
        for i in range(3):
            w1_copy(i).wait_send()

    ag_copy.wait_send()
    st_copy.wait_send()
    nb_copy.wait_send()

    @pl.loop(1, 32)
    def _(d):
        b_copy(d).wait_send()

    for s in range(4):
        for i in range(2):
            x_own(s, i).wait_send()
            x_fwd(s, i).wait_send()
        for i in range(4):
            to_sib(s, i).wait_send()

    @pl.loop(1, 64)
    def _(d):
        c_copy(d % 32, (zh + d // 32) % 2).wait_send()

    mine.wait()
    for dx in (1, 3, 2):
        o_copy(dx).wait_send()
    for dx in (1, 3, 2):
        dst = out.at[:, pl.ds(aligned((x + 4 - dx) % 4, XCOLS), XCOLS)]
        src = rb.at[pl.ds(0, TOK), :]
        remote(src, dst, o_send.at[dx], o_recv.at[dx], z_dev).wait_recv()


def local(spatial_q, spatial_k, spatial_v, norm_gain, temporal_weight):
    dma = pltpu.SemaphoreType.DMA
    flat = [a.reshape(TOK, D) for a in (spatial_q, spatial_k, spatial_v)]
    hbm = pl.BlockSpec(memory_space=pl.ANY)
    out = pl.pallas_call(
        kernel,
        out_shape=jax.ShapeDtypeStruct((TOK, D), BF16),
        in_specs=[hbm, hbm, hbm, pl.BlockSpec(memory_space=pltpu.VMEM), hbm],
        out_specs=hbm,
        scratch_shapes=[
            pltpu.VMEM((HALF_TOK, XCOLS), BF16),
            pltpu.VMEM((HALF_TOK, XCOLS), BF16),
            pltpu.VMEM((HALF_TOK, XCOLS), BF16),
            pltpu.VMEM((2, 64, XCOLS), BF16),
            pltpu.VMEM((XHEADS, HALF_TOK, 128), F32),
            pltpu.VMEM((XHEADS, 128, HALF_TOK), BF16),
            pltpu.VMEM((2, XHEADS, 128, HEAD), BF16),
            pltpu.VMEM((2, 16, 128), F32),
            pltpu.VMEM((HALF_TOK, XCOLS), BF16),
            pltpu.VMEM((3, D, NCOLS), BF16),
            pltpu.VMEM((D, 3 * NCOLS), BF16),
            pltpu.VMEM((2, 4, HALF_TOK, XCOLS), BF16),
            pltpu.VMEM((3 * NHEADS, 1024, HEAD), F32),
            pltpu.VMEM((1024, 128), F32),
            pltpu.VMEM((NHEADS, 1024, HEAD), F32),
            pltpu.VMEM((1024, NCOLS), BF16),
            pltpu.VMEM((HALF_TOK, XCOLS), BF16),
            dma((3, 4)), dma((3, 4)), dma((3,)),
            dma((3,)), dma((3,)),
            dma, dma((3,)), dma((3,)), dma((3, 4)), dma((3, 4)),
            dma((32,)), dma((32,)), dma,
            dma((4, 4)), dma((4, 4)),
            dma((4, 4)), dma((4, 4)),
            dma((2, 32)), dma((2, 32)), dma,
            dma((4,)), dma((4,)), dma,
        ],
        compiler_params=pltpu.CompilerParams(has_side_effects=True, vmem_limit_bytes=56 << 20),
    )(*flat, norm_gain.reshape(D // 128, 128), temporal_weight.transpose(1, 0, 2))
    return out.reshape(1, TOK, D)


def solution(mesh):
    return jax.shard_map(
        local,
        mesh=mesh,
        in_specs=(
            P("frame", "row", None),
            P("frame", "row", None),
            P("frame", "row", None),
            P(),
            P(None, None, "row"),
        ),
        out_specs=P("frame", "row", None),
        check_vma=False,
    )
```

```python
import jax
import jax.numpy as jnp
from jax import lax
from jax.experimental import pallas as pl
from jax.experimental.pallas import tpu as pltpu
from jax.sharding import PartitionSpec as P

D = 3072
HEAD = 128
TOK = 128
XCOLS = D // 4
XHEADS = XCOLS // HEAD
HALF_TOK = 4 * TOK
LOC = 16
NCOLS = D // 8
NHEADS = NCOLS // HEAD
SCALE = HEAD ** (-0.5)
EPS = 1e-06
F32 = jnp.float32
BF16 = jnp.bfloat16
MESH = pl.DeviceIdType.MESH


def aligned(i, n):
    return pl.multiple_of(i * n, n)


def kernel(
    q_hbm, k_hbm, v_hbm, gain, w_hbm, out,
    qx, kx, vx, ag, tw, pb, nb, st, sb, wv, ws, xb, acc, ssq, of, ob, rb,
    a_send, a_recv, a_loc, z_send, z_recv, w_loc, w1_send, w1_recv, wi_send, w2_send, w2_recv,
    b_send, b_recv, b_loc, x_send, x_recv, s_send, s_recv, c_send, c_recv, c_loc, o_send, o_recv, o_loc,
):
    f = lax.axis_index("frame")
    r = lax.axis_index("row")
    zl, y, c = f // 8, (f // 2) % 4, f % 2
    x, zh = r // 2, r % 2

    def dev(zl_, y_, c_, x_, zh_):
        return ((zl_ * 4 + y_) * 2 + c_, x_ * 2 + zh_)

    def remote(src, dst, ss, rs, to):
        return pltpu.make_async_remote_copy(src, dst, ss, rs, device_id=to, device_id_type=MESH)

    z_dev = dev(zl, y, c, x, 1 - zh)
    sib = dev(zl, y, 1 - c, x, zh)
    owner = c == zh

    barrier = pltpu.get_barrier_semaphore()
    for dx in (1, 3, 2):
        pl.semaphore_signal(barrier, inc=1, device_id=dev(zl, y, c, (x + dx) % 4, zh), device_id_type=MESH)

    @pl.loop(1, 64)
    def _(d):
        to = dev((zl + d // 16) % 4, (y + (d // 4) % 4) % 4, (c + d % 2) % 2, x, (zh + (d // 2) % 2) % 2)
        pl.semaphore_signal(barrier, inc=1, device_id=to, device_id_type=MESH)

    half_cols = XCOLS // 2
    parts = ((q_hbm, qx, 0, XCOLS), (k_hbm, kx, 0, XCOLS), (v_hbm, vx, 0, half_cols), (v_hbm, vx, half_cols, half_cols))

    def a_from(t, xp):
        src, _, lo, n = parts[t]
        return src.at[:, pl.ds(pl.multiple_of(xp * XCOLS + lo, 128), n)]

    def a_to(t):
        _, dst, lo, n = parts[t]
        return dst.at[pl.ds(aligned(x, TOK), TOK), pl.ds(lo, n)]

    def a_copy(t, dx):
        xp = (x + dx) % 4
        return remote(a_from(t, xp), a_to(t), a_send.at[t, dx], a_recv.at[t, dx], dev(zl, y, c, xp, zh))

    def a_local(t):
        return pltpu.make_async_copy(a_from(t, x), a_to(t), a_loc.at[t])

    def a_wait(t):
        for dx in (1, 3, 2):
            a_copy(t, dx).wait_recv()
        a_local(t).wait()

    edge = jnp.logical_or(zl == 0, zl == 3)
    away = jnp.logical_not(owner)

    def piece(y_, p):
        return ws.at[pl.ds(pl.multiple_of(y_ * 768 + p * 128, 128), 128), :]

    def w1_copy(p):
        return remote(piece(y, p), piece(y, p), w1_send.at[p], w1_recv.at[p], dev(3 - zl, y, c, x, 1 - zh))

    def wi_copy(p):
        to = dev(1 + zl // 3, y, c, x, zh)
        return remote(piece(y, p), piece(y, p), wi_send.at[p], w1_recv.at[p], to)

    def w2_copy(p, dy):
        to = dev(zl, (y + dy) % 4, c, x, zh)
        return remote(piece(y, p), piece(y, p), w2_send.at[p, dy], w2_recv.at[p, dy], to)

    def w_forward(point):
        def some(first, inner):
            for p in (first, first + 1):
                w1_copy(p).wait_recv()
                if not inner:
                    wi_copy(p).start()
                for dy in (1, 3, 2):
                    w2_copy(p, dy).start()

        if point < 3:

            @pl.when(jnp.logical_and(away, edge))
            def _():
                some(2 * point, False)

        if point > 0:

            @pl.when(jnp.logical_and(away, jnp.logical_not(edge)))
            def _():
                some(2 * point - 2, True)

    def w_scale(first, last):
        @pl.loop(first, last)
        def _(i):
            kc = (y * 6 + i) % 24
            g = jnp.broadcast_to(gain[pl.ds(kc, 1), :], (128, 128)).T
            rows = pl.ds(aligned(kc, 128), 128)
            for i in range(3):
                for j in range(NHEADS):
                    scaled = wv[i, rows, j * HEAD : (j + 1) * HEAD].astype(F32) * g
                    ws[rows, i * NCOLS + j * HEAD : i * NCOLS + (j + 1) * HEAD] = scaled.astype(BF16)

    for t in range(4):
        a_local(t).start()

    @pl.when(owner)
    def _():
        load = pltpu.make_async_copy(w_hbm, wv, w_loc)
        load.start()
        load.wait()
        w_scale(0, 6)

    pl.semaphore_wait(barrier, 66)
    for t in range(4):
        for dx in (1, 3, 2):
            a_copy(t, dx).start()

    @pl.when(jnp.logical_and(owner, edge))
    def _():
        for p in range(6):
            w1_copy(p).start()

    @pl.when(owner)
    def _():
        w_scale(6, 24)

    a_wait(0)
    pool = (
        lax.broadcasted_iota(jnp.int32, (64, HALF_TOK), 1) // 8 == lax.broadcasted_iota(jnp.int32, (64, HALF_TOK), 0)
    ).astype(F32) * 0.125
    ag[zh] = jnp.dot(pool.astype(BF16), qx[...], preferred_element_type=F32).astype(BF16)
    ag_copy = remote(ag.at[zh], ag.at[zh], z_send.at[0], z_recv.at[0], z_dev)
    ag_copy.start()
    w_forward(0)
    ag_copy.wait_recv()

    def nt(a, b):
        return lax.dot_general(a, b, (((1,), (1,)), ((), ())), preferred_element_type=F32)

    def head(h):
        return slice(h * HEAD, (h + 1) * HEAD)

    def agents(h):
        return ag[:, :, head(h)].reshape(2 * 64, HEAD)

    for h in range(XHEADS):
        s = nt(qx[:, head(h)], agents(h)) * SCALE
        e = jnp.exp(s - jnp.max(s, axis=1, keepdims=True))
        tw[h] = e * (1.0 / jnp.sum(e, axis=1, keepdims=True))
    w_forward(1)

    a_wait(1)
    lane = lax.broadcasted_iota(jnp.int32, (128, 128), 1)
    stats = jnp.where(lane < 8, 0.0, 1.0)
    for h in range(XHEADS):
        s = nt(agents(h), kx[:, head(h)]) * SCALE
        m = jnp.max(s, axis=1, keepdims=True)
        e = jnp.exp(s - m)
        pb[h] = e.astype(BF16)
        stats = jnp.where(lane == h, m, stats)
        stats = jnp.where(lane == 8 + h, jnp.sum(e, axis=1, keepdims=True), stats)
    st[zh] = stats.T[0:16, :]
    st_copy = remote(st.at[zh], st.at[zh], z_send.at[1], z_recv.at[1], z_dev)
    st_copy.start()
    w_forward(2)

    def nb_copy(i):
        half = nb.at[zh, 3 * i : 3 * i + 3]
        return remote(half, half, z_send.at[2 + i], z_recv.at[2 + i], z_dev)

    for i in range(2):
        a_wait(2 + i)
        for h in range(3 * i, 3 * i + 3):
            nb[zh, h] = jnp.dot(pb[h], vx[:, head(h)], preferred_element_type=F32).astype(BF16)
        nb_copy(i).start()
    st_copy.wait_recv()
    m0, m1 = st[0, 0:8, :], st[1, 0:8, :]
    l0, l1 = st[0, 8:16, :], st[1, 8:16, :]
    peak = jnp.maximum(m0, m1)
    e0, e1 = jnp.exp(m0 - peak), jnp.exp(m1 - peak)
    inv = 1.0 / (l0 * e0 + l1 * e1)
    s0, s1 = e0 * inv, e1 * inv
    w_forward(3)

    for h in range(XHEADS):
        if h % 3 == 0:
            nb_copy(h // 3).wait_recv()
        t = tw[h]
        both = jnp.concatenate([(t * s0[h : h + 1, :]).astype(BF16), (t * s1[h : h + 1, :]).astype(BF16)], axis=1)
        sb[:, head(h)] = jnp.dot(
            both, nb[:, h].reshape(256, HEAD), preferred_element_type=F32
        ).astype(BF16)

    me = (zl * 4 + y) * 2 + zh

    def b_copy(d):
        zl_, y_, zh_ = (zl + d // 8) % 4, (y + (d // 2) % 4) % 4, (zh + d % 2) % 2
        g = y_ * 8 + zh_ * 4 + zl_
        return remote(
            sb.at[pl.ds(aligned(g, LOC), LOC), :],
            xb.at[c, x, pl.ds(aligned(me, LOC), LOC), :],
            b_send.at[d], b_recv.at[d], dev(zl_, y_, c, x, zh_),
        )

    def b_wait(d):
        zl_, y_, zh_ = (zl + 4 - d // 8) % 4, (y + 4 - (d // 2) % 4) % 4, (zh + d % 2) % 2
        row = (zl_ * 4 + y_) * 2 + zh_
        dst = xb.at[c, x, pl.ds(aligned(row, LOC), LOC), :]
        remote(dst, dst, b_send.at[d], b_recv.at[d], z_dev).wait_recv()

    group = y * 8 + zh * 4 + zl
    own = pltpu.make_async_copy(
        sb.at[pl.ds(aligned(group, LOC), LOC), :], xb.at[c, x, pl.ds(aligned(me, LOC), LOC), :], b_loc
    )
    own.start()

    @pl.loop(1, 32)
    def _(d):
        b_copy(d).start()

    @pl.when(away)
    def _():
        for p in range(6):
            for dy in (1, 3, 2):
                dst = piece((y + 4 - dy) % 4, p)
                remote(dst, dst, w2_send.at[p, dy], w2_recv.at[p, dy], z_dev).wait_recv()

    left, right, far = (x + 3) % 4, (x + 1) % 4, (x + 2) % 4

    def block(half, col, s, lo=0, n=128):
        zl_ = (zl + 4 - s) % 4
        return xb.at[half, col, pl.ds(pl.multiple_of(zl_ * 128 + lo, 64), n), :]

    def x_own(s, i):
        b = block(c, x, s)
        return remote(b, b, x_send.at[s, i], x_recv.at[s, i], dev(zl, y, c, (right, left)[i], zh))

    def x_fwd(s, i):
        b = block(c, (left, right)[i], s, 64 * i, 64)
        return remote(b, b, x_send.at[s, 2 + i], x_recv.at[s, 2 + i], dev(zl, y, c, (right, left)[i], zh))

    def x_got(s, i):
        col = (left, right, far, far)[i]
        b = block(c, col, s, *((0, 128), (0, 128), (0, 64), (64, 64))[i])
        return remote(b, b, x_send.at[s, i], x_recv.at[s, i], z_dev)

    def to_sib(s, i):
        b = block(c, (x, left, right, far)[i], s)
        return remote(b, b, s_send.at[s, i], s_recv.at[s, i], sib)

    def from_sib(s, i):
        b = block(1 - c, (x, left, right, far)[i], s)
        return remote(b, b, s_send.at[s, i], s_recv.at[s, i], sib)

    def mm(half, col, first=False):
        rows_w = pl.ds(aligned(col, XCOLS), XCOLS)

        @pl.loop(0, 2)
        def _(i):
            src = xb[half, col, pl.ds(aligned(i, 256), 256), :]
            rows = pl.ds(pl.multiple_of(half * 512 + i * 256, 256), 256)
            p = jnp.dot(src, ws[rows_w, :], preferred_element_type=F32)
            wide = src.astype(F32)
            sq = jnp.broadcast_to(jnp.sum(wide * wide, axis=1, keepdims=True), (256, 128))
            for j in range(3 * NHEADS):
                if first:
                    acc[j, rows, :] = p[:, head(j)]
                else:
                    acc[j, rows, :] += p[:, head(j)]
            if first:
                ssq[rows, :] = sq
            else:
                ssq[rows, :] += sq

    for s in range(6):
        if s < 4:
            if s == 0:
                own.wait()
            for d in range(8 * s, 8 * s + 8):
                if d:
                    b_wait(d)
            x_own(s, 0).start()
            x_own(s, 1).start()
            to_sib(s, 0).start()
        if 1 <= s < 5:
            for i in range(2):
                x_got(s - 1, i).wait_recv()
                x_fwd(s - 1, i).start()
                to_sib(s - 1, 1 + i).start()
        if s == 3:
            mm(c, x, True)
        if s == 4:
            for q in range(4):
                from_sib(q, 0).wait_recv()
            mm(1 - c, x, True)
        if s == 5:
            for q in range(4):
                from_sib(q, 1).wait_recv()
                from_sib(q, 2).wait_recv()
            mm(1 - c, left)
            mm(1 - c, right)
        if s >= 2:
            for i in (2, 3):
                x_got(s - 2, i).wait_recv()
            to_sib(s - 2, 3).start()
        if s == 4:
            mm(c, left)
            mm(c, right)
    mm(c, far)
    for q in range(4):
        from_sib(q, 3).wait_recv()
    mm(1 - c, far)
    ssq[...] = lax.rsqrt(ssq[...] * (1.0 / D) + EPS)

    same = (
        lax.broadcasted_iota(jnp.int32, (128, 128), 0) // 32 == lax.broadcasted_iota(jnp.int32, (128, 128), 1) // 32
    )

    def c_copy(d, h):
        zl_, y_, c_ = (zl + d // 8) % 4, (y + (d // 2) % 4) % 4, (c + d % 2) % 2
        row = c_ * 512 + (zl_ * 4 + y_) * 32 + h * LOC
        hs = (h + 2 - zh) % 2
        return remote(
            ob.at[pl.ds(pl.multiple_of(row, LOC), LOC), :],
            rb.at[pl.ds(aligned(group, LOC), LOC), pl.ds(aligned(c, NCOLS), NCOLS)],
            c_send.at[hs, d], c_recv.at[hs, d], dev(zl_, y_, c_, x, h),
        )

    def c_own():
        row = c * 512 + (zl * 4 + y) * 32 + zh * LOC
        return pltpu.make_async_copy(
            ob.at[pl.ds(pl.multiple_of(row, LOC), LOC), :],
            rb.at[pl.ds(aligned(group, LOC), LOC), pl.ds(aligned(c, NCOLS), NCOLS)], c_loc,
        )

    def attend(picks):
        norm = jnp.concatenate([ssq[p, :] for p in picks], axis=0)

        def rows_of(j):
            return (jnp.concatenate([acc[j, p, :] for p in picks], axis=0) * norm).astype(BF16)

        for h in range(NHEADS):
            s = nt(rows_of(h), rows_of(NHEADS + h)) * SCALE
            s = jnp.where(same, s, -1e30)
            e = jnp.exp(s - jnp.max(s, axis=1, keepdims=True))
            p = (e * (1.0 / jnp.sum(e, axis=1, keepdims=True))).astype(BF16)
            o = jnp.dot(p, rows_of(2 * NHEADS + h), preferred_element_type=F32)
            for i in range(4):
                of[h, picks[i], :] = o[32 * i : 32 * i + 32, :]

    for part in range(2):

        @pl.loop(part * 2, part * 2 + 2)
        def _(b2):
            for b in (2 * b2, 2 * b2 + 1):
                attend([pl.ds(b * 4 + i, 32, stride=32) for i in range(4)])

        @pl.loop(0, 32)
        def _(k):
            rows = pl.ds(pl.multiple_of(k * 32 + part * LOC, LOC), LOC)
            for h in range(NHEADS):
                ob[rows, head(h)] = of[h, rows, :].astype(BF16)

        @pl.loop(1, 32)
        def _(d):
            c_copy(d, part).start()

        @pl.when(zh == part)
        def _():
            c_own().start()

        @pl.when(zh != part)
        def _():
            c_copy(0, part).start()

    def c_wait(xs):
        @pl.loop(0, 16)
        def _(i):
            dz, hs, dc = i // 4, (i // 2) % 2, i % 2
            dy = (y + 4 - xs) % 4
            d = dz * 8 + dy * 2 + dc
            g = xs * 8 + ((zh + hs) % 2) * 4 + (zl + 4 - dz) % 4
            dst = rb.at[pl.ds(aligned(g, LOC), LOC), pl.ds(aligned((c + dc) % 2, NCOLS), NCOLS)]

            @pl.when(d + hs > 0)
            def _():
                remote(dst, dst, c_send.at[hs, d], c_recv.at[hs, d], z_dev).wait_recv()

            @pl.when(d + hs == 0)
            def _():
                c_own().wait()

    def o_copy(dx):
        xp = (x + dx) % 4
        return remote(
            rb.at[pl.ds(aligned(xp, TOK), TOK), :], out.at[:, pl.ds(aligned(x, XCOLS), XCOLS)],
            o_send.at[dx], o_recv.at[dx], dev(zl, y, c, xp, zh),
        )

    for dx in (1, 3, 2):
        c_wait((x + dx) % 4)
        o_copy(dx).start()
    c_wait(x)
    mine = pltpu.make_async_copy(
        rb.at[pl.ds(aligned(x, TOK), TOK), :], out.at[:, pl.ds(aligned(x, XCOLS), XCOLS)], o_loc
    )
    mine.start()

    for t in range(4):
        for dx in (1, 3, 2):
            a_copy(t, dx).wait_send()

    @pl.when(jnp.logical_and(owner, edge))
    def _():
        for p in range(6):
            w1_copy(p).wait_send()

    @pl.when(jnp.logical_and(away, edge))
    def _():
        for p in range(6):
            wi_copy(p).wait_send()

    @pl.when(away)
    def _():
        for p in range(6):
            for dy in (1, 3, 2):
                w2_copy(p, dy).wait_send()

    ag_copy.wait_send()
    st_copy.wait_send()
    for i in range(2):
        nb_copy(i).wait_send()

    @pl.loop(1, 32)
    def _(d):
        b_copy(d).wait_send()

    for s in range(4):
        for i in range(2):
            x_own(s, i).wait_send()
            x_fwd(s, i).wait_send()
        for i in range(4):
            to_sib(s, i).wait_send()

    @pl.loop(1, 64)
    def _(d):
        c_copy(d % 32, (zh + d // 32) % 2).wait_send()

    mine.wait()
    for dx in (1, 3, 2):
        o_copy(dx).wait_send()
    for dx in (1, 3, 2):
        dst = out.at[:, pl.ds(aligned((x + 4 - dx) % 4, XCOLS), XCOLS)]
        src = rb.at[pl.ds(0, TOK), :]
        remote(src, dst, o_send.at[dx], o_recv.at[dx], z_dev).wait_recv()


def local(spatial_q, spatial_k, spatial_v, norm_gain, temporal_weight):
    dma = pltpu.SemaphoreType.DMA
    flat = [a.reshape(TOK, D) for a in (spatial_q, spatial_k, spatial_v)]
    hbm = pl.BlockSpec(memory_space=pl.ANY)
    out = pl.pallas_call(
        kernel,
        out_shape=jax.ShapeDtypeStruct((TOK, D), BF16),
        in_specs=[hbm, hbm, hbm, pl.BlockSpec(memory_space=pltpu.VMEM), hbm],
        out_specs=hbm,
        scratch_shapes=[
            pltpu.VMEM((HALF_TOK, XCOLS), BF16),
            pltpu.VMEM((HALF_TOK, XCOLS), BF16),
            pltpu.VMEM((HALF_TOK, XCOLS), BF16),
            pltpu.VMEM((2, 64, XCOLS), BF16),
            pltpu.VMEM((XHEADS, HALF_TOK, 128), F32),
            pltpu.VMEM((XHEADS, 128, HALF_TOK), BF16),
            pltpu.VMEM((2, XHEADS, 128, HEAD), BF16),
            pltpu.VMEM((2, 16, 128), F32),
            pltpu.VMEM((HALF_TOK, XCOLS), BF16),
            pltpu.VMEM((3, D, NCOLS), BF16),
            pltpu.VMEM((D, 3 * NCOLS), BF16),
            pltpu.VMEM((2, 4, HALF_TOK, XCOLS), BF16),
            pltpu.VMEM((3 * NHEADS, 1024, HEAD), F32),
            pltpu.VMEM((1024, 128), F32),
            pltpu.VMEM((NHEADS, 1024, HEAD), F32),
            pltpu.VMEM((1024, NCOLS), BF16),
            pltpu.VMEM((HALF_TOK, XCOLS), BF16),
            dma((4, 4)), dma((4, 4)), dma((4,)),
            dma((4,)), dma((4,)),
            dma, dma((6,)), dma((6,)), dma((6,)), dma((6, 4)), dma((6, 4)),
            dma((32,)), dma((32,)), dma,
            dma((4, 4)), dma((4, 4)),
            dma((4, 4)), dma((4, 4)),
            dma((2, 32)), dma((2, 32)), dma,
            dma((4,)), dma((4,)), dma,
        ],
        compiler_params=pltpu.CompilerParams(collective_id=0, has_side_effects=True, vmem_limit_bytes=56 << 20),
    )(*flat, norm_gain.reshape(D // 128, 128), temporal_weight.transpose(1, 0, 2))
    return out.reshape(1, TOK, D)


def solution(mesh):
    return jax.shard_map(
        local,
        mesh=mesh,
        in_specs=(
            P("frame", "row", None),
            P("frame", "row", None),
            P("frame", "row", None),
            P(),
            P(None, None, "row"),
        ),
        out_specs=P("frame", "row", None),
        check_vma=False,
    )
```

```python
import jax
import jax.numpy as jnp
from jax import lax
from jax.experimental import pallas as pl
from jax.experimental.pallas import tpu as pltpu
from jax.sharding import PartitionSpec as P

D = 3072
HEAD = 128
TOK = 128
XCOLS = D // 4
XHEADS = XCOLS // HEAD
HALF_TOK = 4 * TOK
LOC = 16
NCOLS = D // 8
NHEADS = NCOLS // HEAD
SCALE = HEAD ** (-0.5)
EPS = 1e-06
F32 = jnp.float32
BF16 = jnp.bfloat16
MESH = pl.DeviceIdType.MESH


def aligned(i, n):
    return pl.multiple_of(i * n, n)


def kernel(
    q_hbm, k_hbm, v_hbm, gain, w_hbm, out,
    qx, kx, vx, ag, tw, pb, nb, st, sb, wv, ws, xb, acc, ssq, ob, rb,
    a_send, a_recv, a_loc, z_send, z_recv, w_loc, w1_send, w1_recv, wi_send, w2_send, w2_recv,
    b_send, b_recv, b_loc, x_send, x_recv, s_send, s_recv, c_send, c_recv, c_loc, o_send, o_recv, o_loc,
):
    f = lax.axis_index("frame")
    r = lax.axis_index("row")
    zl, y, c = f // 8, (f // 2) % 4, f % 2
    x, zh = r // 2, r % 2

    def dev(zl_, y_, c_, x_, zh_):
        return ((zl_ * 4 + y_) * 2 + c_, x_ * 2 + zh_)

    def remote(src, dst, ss, rs, to):
        return pltpu.make_async_remote_copy(src, dst, ss, rs, device_id=to, device_id_type=MESH)

    z_dev = dev(zl, y, c, x, 1 - zh)
    sib = dev(zl, y, 1 - c, x, zh)
    owner = c == zh

    barrier = pltpu.get_barrier_semaphore()
    for dx in (1, 3, 2):
        pl.semaphore_signal(barrier, inc=1, device_id=dev(zl, y, c, (x + dx) % 4, zh), device_id_type=MESH)

    for d in range(63, 0, -1):
        to = dev((zl + d // 16) % 4, (y + (d // 4) % 4) % 4, (c + d % 2) % 2, x, (zh + (d // 2) % 2) % 2)
        pl.semaphore_signal(barrier, inc=1, device_id=to, device_id_type=MESH)

    half_cols = XCOLS // 2
    parts = ((q_hbm, qx, 0, XCOLS), (k_hbm, kx, 0, XCOLS), (v_hbm, vx, 0, half_cols), (v_hbm, vx, half_cols, half_cols))

    def a_from(t, xp):
        src, _, lo, n = parts[t]
        return src.at[:, pl.ds(pl.multiple_of(xp * XCOLS + lo, 128), n)]

    def a_to(t):
        _, dst, lo, n = parts[t]
        return dst.at[pl.ds(aligned(x, TOK), TOK), pl.ds(lo, n)]

    def a_copy(t, dx):
        xp = (x + dx) % 4
        return remote(a_from(t, xp), a_to(t), a_send.at[t, dx], a_recv.at[t, dx], dev(zl, y, c, xp, zh))

    def a_local(t):
        return pltpu.make_async_copy(a_from(t, x), a_to(t), a_loc.at[t])

    def a_wait(t):
        for dx in (1, 3, 2):
            a_copy(t, dx).wait_recv()
        a_local(t).wait()

    edge = jnp.logical_or(zl == 0, zl == 3)
    away = jnp.logical_not(owner)

    def piece(y_, p):
        return ws.at[pl.ds(pl.multiple_of(y_ * 768 + p * 128, 128), 128), :]

    def w1_copy(p):
        return remote(piece(y, p), piece(y, p), w1_send.at[p], w1_recv.at[p], dev(3 - zl, y, c, x, 1 - zh))

    def wi_copy(p):
        to = dev(1 + zl // 3, y, c, x, zh)
        return remote(piece(y, p), piece(y, p), wi_send.at[p], w1_recv.at[p], to)

    def w2_copy(p, dy):
        to = dev(zl, (y + dy) % 4, c, x, zh)
        return remote(piece(y, p), piece(y, p), w2_send.at[p, dy], w2_recv.at[p, dy], to)

    def w_forward(outer, inner):
        def some(pieces, behind):
            for p in pieces:
                w1_copy(p).wait_recv()
                if behind:
                    wi_copy(p).start()
                for dy in (1, 3, 2):
                    w2_copy(p, dy).start()

        if outer:

            @pl.when(jnp.logical_and(away, edge))
            def _():
                some(outer, True)

        if inner:

            @pl.when(jnp.logical_and(away, jnp.logical_not(edge)))
            def _():
                some(inner, False)

    def w_scale(first, last):
        @pl.loop(first, last)
        def _(i):
            kc = (y * 6 + i) % 24
            g = jnp.broadcast_to(gain[pl.ds(kc, 1), :], (128, 128)).T
            rows = pl.ds(aligned(kc, 128), 128)
            for i in range(3):
                for j in range(NHEADS):
                    scaled = wv[i, rows, j * HEAD : (j + 1) * HEAD].astype(F32) * g
                    ws[rows, i * NCOLS + j * HEAD : i * NCOLS + (j + 1) * HEAD] = scaled.astype(BF16)

    for t in range(4):
        a_local(t).start()

    @pl.when(owner)
    def _():
        load = pltpu.make_async_copy(w_hbm, wv, w_loc)
        load.start()
        load.wait()
        w_scale(0, 6)

    pl.semaphore_wait(barrier, 66)
    for t in range(4):
        for dx in (1, 3, 2):
            a_copy(t, dx).start()

    @pl.when(jnp.logical_and(owner, edge))
    def _():
        for p in range(6):
            w1_copy(p).start()

    @pl.when(owner)
    def _():
        w_scale(6, 24)

    w_forward((0, 1), ())
    a_wait(0)
    pool = (
        lax.broadcasted_iota(jnp.int32, (64, HALF_TOK), 1) // 8 == lax.broadcasted_iota(jnp.int32, (64, HALF_TOK), 0)
    ).astype(F32) * 0.125
    ag[zh] = jnp.dot(pool.astype(BF16), qx[...], preferred_element_type=F32).astype(BF16)
    ag_copy = remote(ag.at[zh], ag.at[zh], z_send.at[0], z_recv.at[0], z_dev)
    ag_copy.start()
    w_forward((2, 3), (0,))
    ag_copy.wait_recv()
    w_forward((4, 5), (1, 2))

    def nt(a, b):
        return lax.dot_general(a, b, (((1,), (1,)), ((), ())), preferred_element_type=F32)

    def head(h):
        return slice(h * HEAD, (h + 1) * HEAD)

    def agents(h):
        return ag[:, :, head(h)].reshape(2 * 64, HEAD)

    for h in range(XHEADS):
        s = nt(qx[:, head(h)], agents(h)) * SCALE
        e = jnp.exp(s - jnp.max(s, axis=1, keepdims=True))
        tw[h] = e * (1.0 / jnp.sum(e, axis=1, keepdims=True))
    w_forward((), (3,))

    a_wait(1)
    lane = lax.broadcasted_iota(jnp.int32, (128, 128), 1)
    stats = jnp.where(lane < 8, 0.0, 1.0)
    for h in range(XHEADS):
        s = nt(agents(h), kx[:, head(h)]) * SCALE
        m = jnp.max(s, axis=1, keepdims=True)
        e = jnp.exp(s - m)
        pb[h] = e.astype(BF16)
        stats = jnp.where(lane == h, m, stats)
        stats = jnp.where(lane == 8 + h, jnp.sum(e, axis=1, keepdims=True), stats)
    st[zh] = stats.T[0:16, :]
    st_copy = remote(st.at[zh], st.at[zh], z_send.at[1], z_recv.at[1], z_dev)
    st_copy.start()
    w_forward((), (4, 5))

    def nb_copy(i):
        half = nb.at[zh, 3 * i : 3 * i + 3]
        return remote(half, half, z_send.at[2 + i], z_recv.at[2 + i], z_dev)

    for i in range(2):
        a_wait(2 + i)
        for h in range(3 * i, 3 * i + 3):
            nb[zh, h] = jnp.dot(pb[h], vx[:, head(h)], preferred_element_type=F32).astype(BF16)
        nb_copy(i).start()
    st_copy.wait_recv()
    m0, m1 = st[0, 0:8, :], st[1, 0:8, :]
    l0, l1 = st[0, 8:16, :], st[1, 8:16, :]
    peak = jnp.maximum(m0, m1)
    e0, e1 = jnp.exp(m0 - peak), jnp.exp(m1 - peak)
    inv = 1.0 / (l0 * e0 + l1 * e1)
    s0, s1 = e0 * inv, e1 * inv

    for h in range(XHEADS):
        if h % 3 == 0:
            nb_copy(h // 3).wait_recv()
        t = tw[h]
        both = jnp.concatenate([(t * s0[h : h + 1, :]).astype(BF16), (t * s1[h : h + 1, :]).astype(BF16)], axis=1)
        sb[:, head(h)] = jnp.dot(
            both, nb[:, h].reshape(256, HEAD), preferred_element_type=F32
        ).astype(BF16)

    z = zh * 4 + zl
    me = z * 4 + y

    def nearest(step):
        return (step % 2) * ((step + 1) // 2) + (1 - step % 2) * ((8 - step // 2) % 8)

    def b_copy(n):
        z_, y_ = (z + nearest(n // 4)) % 8, (y + n % 4) % 4
        return remote(
            sb.at[pl.ds(aligned(y_ * 8 + z_, LOC), LOC), :],
            xb.at[c, x, pl.ds(aligned(me, LOC), LOC), :],
            b_send.at[n], b_recv.at[n], dev(z_ % 4, y_, c, x, z_ // 4),
        )

    def b_wait(n):
        z_, y_ = (z + 8 - nearest(n // 4)) % 8, (y + 4 - n % 4) % 4
        dst = xb.at[c, x, pl.ds(aligned(z_ * 4 + y_, LOC), LOC), :]
        remote(dst, dst, b_send.at[n], b_recv.at[n], z_dev).wait_recv()

    group = y * 8 + z
    own = pltpu.make_async_copy(
        sb.at[pl.ds(aligned(group, LOC), LOC), :], xb.at[c, x, pl.ds(aligned(me, LOC), LOC), :], b_loc
    )
    own.start()

    @pl.loop(1, 32)
    def _(n):
        b_copy(n).start()

    left, right, far = (x + 3) % 4, (x + 1) % 4, (x + 2) % 4

    def block(half, col, s, lo=0, n=64):
        z_ = (z + 8 - nearest(s)) % 8
        return xb.at[half, col, pl.ds(pl.multiple_of(z_ * 64 + lo, 32), n), :]

    def x_own(s, i):
        b = block(c, x, s)
        return remote(b, b, x_send.at[s, i], x_recv.at[s, i], dev(zl, y, c, (right, left)[i], zh))

    def x_fwd(s, i):
        b = block(c, (left, right)[i], s, 32 * i, 32)
        return remote(b, b, x_send.at[s, 2 + i], x_recv.at[s, 2 + i], dev(zl, y, c, (right, left)[i], zh))

    def x_got(s, i):
        col = (left, right, far, far)[i]
        b = block(c, col, s, *((0, 64), (0, 64), (0, 32), (32, 32))[i])
        return remote(b, b, x_send.at[s, i], x_recv.at[s, i], z_dev)

    def to_sib(s, i):
        b = block(c, (x, left, right, far)[i], s)
        return remote(b, b, s_send.at[s, i], s_recv.at[s, i], sib)

    def from_sib(s, i):
        b = block(1 - c, (x, left, right, far)[i], s)
        return remote(b, b, s_send.at[s, i], s_recv.at[s, i], sib)

    def mm(half, col, first=False):
        rows_w = pl.ds(aligned(col, XCOLS), XCOLS)

        @pl.loop(0, 2)
        def _(i):
            src = xb[half, col, pl.ds(aligned(i, 256), 256), :]
            p = jnp.dot(src, ws[rows_w, :], preferred_element_type=F32)
            wide = src.astype(F32)
            sq = jnp.broadcast_to(jnp.sum(wide * wide, axis=1, keepdims=True), (256, 128)).reshape(16, LOC, 128)
            for j in range(3 * NHEADS):
                pj = p[:, head(j)].reshape(16, LOC, 128)
                if first:
                    acc[j, half, i] = pj
                else:
                    acc[j, half, i] += pj
            if first:
                ssq[half, i] = sq
            else:
                ssq[half, i] += sq

    def sides(s):
        for i in range(2):
            x_got(s, i).wait_recv()
            x_fwd(s, i).start()
            to_sib(s, 1 + i).start()

    def ends(s):
        x_got(s, 2).wait_recv()
        x_got(s, 3).wait_recv()
        to_sib(s, 3).start()

    for s in range(8):
        if s == 0:
            own.wait()
        for n in range(4 * s, 4 * s + 4):
            if n:
                b_wait(n)
        x_own(s, 0).start()
        x_own(s, 1).start()
        to_sib(s, 0).start()
        if s >= 1:
            sides(s - 1)
        if s >= 2:
            ends(s - 2)

    @pl.when(away)
    def _():
        for p in range(6):
            for dy in (1, 3, 2):
                dst = piece((y + 4 - dy) % 4, p)
                remote(dst, dst, w2_send.at[p, dy], w2_recv.at[p, dy], z_dev).wait_recv()

    mm(c, x, True)
    for s in range(8):
        from_sib(s, 0).wait_recv()
    mm(1 - c, x, True)
    sides(7)
    ends(6)
    mm(c, left)
    mm(c, right)
    for s in range(8):
        from_sib(s, 1).wait_recv()
        from_sib(s, 2).wait_recv()
    mm(1 - c, left)
    ends(7)
    mm(1 - c, right)
    mm(c, far)
    for s in range(8):
        from_sib(s, 3).wait_recv()
    mm(1 - c, far)
    ssq[...] = lax.rsqrt(ssq[...] * (1.0 / D) + EPS)

    same = lax.broadcasted_iota(jnp.int32, (256, 256), 0) % 8 == lax.broadcasted_iota(jnp.int32, (256, 256), 1) % 8

    def attend(zh_, lo):
        norm = ssq[:, zh_, :, lo : lo + 8, :].reshape(256, 128)

        def rows_of(j):
            return (acc[j, :, zh_, :, lo : lo + 8, :].reshape(256, 128) * norm).astype(BF16)

        for h in range(NHEADS):
            s = nt(rows_of(h), rows_of(NHEADS + h)) * SCALE
            s = jnp.where(same, s, -1e30)
            e = jnp.exp(s - jnp.max(s, axis=1, keepdims=True))
            p = (e * (1.0 / jnp.sum(e, axis=1, keepdims=True))).astype(BF16)
            o = jnp.dot(p, rows_of(2 * NHEADS + h), preferred_element_type=F32)
            ob[:, zh_, :, lo : lo + 8, head(h)] = o.astype(BF16).reshape(2, 16, 8, HEAD)

    def c_to(g, c_):
        return rb.at[pl.ds(aligned(g, LOC), LOC), pl.ds(aligned(c_, NCOLS), NCOLS)]

    def c_copy(d, hs):
        zl_, y_, c_, zh_ = (zl + d // 8) % 4, (y + (d // 2) % 4) % 4, (c + d % 2) % 2, (zh + hs) % 2
        src = ob.at[c_, zh_, zl_ * 4 + y_]
        return remote(src, c_to(group, c), c_send.at[hs, d], c_recv.at[hs, d], dev(zl_, y_, c_, x, zh_))

    def c_own():
        return pltpu.make_async_copy(ob.at[c, zh, zl * 4 + y], c_to(group, c), c_loc)

    for hs in (1, 0):
        for lo in (0, 8):
            attend((zh + hs) % 2, lo)

        @pl.loop(1 - hs, 32)
        def _(d):
            c_copy(d, hs).start()

    c_own().start()

    def c_wait(z_, y_, dc):
        d = ((zl + 4 - z_ % 4) % 4) * 8 + ((y + 4 - y_) % 4) * 2 + dc
        hs = (zh + z_ // 4) % 2
        dst = c_to(y_ * 8 + z_, (c + dc) % 2)

        @pl.when(d + hs > 0)
        def _():
            remote(dst, dst, c_send.at[hs, d], c_recv.at[hs, d], z_dev).wait_recv()

        @pl.when(d + hs == 0)
        def _():
            c_own().wait()

    def o_copy(s, dx):
        z_, xp = (z + 8 - nearest(s)) % 8, (x + dx) % 4
        return remote(
            rb.at[pl.ds(aligned(xp * 8 + z_, LOC), LOC), :],
            out.at[pl.ds(aligned(z_, LOC), LOC), pl.ds(aligned(x, XCOLS), XCOLS)],
            o_send.at[s, dx], o_recv.at[s, dx], dev(zl, y, c, xp, zh),
        )

    @pl.loop(0, 8)
    def _(s):
        z_ = (z + 8 - nearest(s)) % 8
        for dx in (1, 3, 2, 0):
            for dc in range(2):
                c_wait(z_, (x + dx) % 4, dc)
            if dx:
                o_copy(s, dx).start()

    mine = pltpu.make_async_copy(
        rb.at[pl.ds(aligned(x, TOK), TOK), :], out.at[:, pl.ds(aligned(x, XCOLS), XCOLS)], o_loc
    )
    mine.start()

    for t in range(4):
        for dx in (1, 3, 2):
            a_copy(t, dx).wait_send()

    @pl.when(jnp.logical_and(owner, edge))
    def _():
        for p in range(6):
            w1_copy(p).wait_send()

    @pl.when(jnp.logical_and(away, edge))
    def _():
        for p in range(6):
            wi_copy(p).wait_send()

    @pl.when(away)
    def _():
        for p in range(6):
            for dy in (1, 3, 2):
                w2_copy(p, dy).wait_send()

    ag_copy.wait_send()
    st_copy.wait_send()
    for i in range(2):
        nb_copy(i).wait_send()

    @pl.loop(1, 32)
    def _(d):
        b_copy(d).wait_send()

    for s in range(8):
        for i in range(2):
            x_own(s, i).wait_send()
            x_fwd(s, i).wait_send()
        for i in range(4):
            to_sib(s, i).wait_send()

    @pl.loop(1, 64)
    def _(d):
        c_copy(d % 32, d // 32).wait_send()

    mine.wait()

    @pl.loop(0, 8)
    def _(s):
        for dx in (1, 3, 2):
            o_copy(s, dx).wait_send()

    @pl.loop(0, 8)
    def _(s):
        z_ = (z + 8 - nearest(s)) % 8
        for dx in (1, 3, 2):
            dst = out.at[pl.ds(aligned(z_, LOC), LOC), pl.ds(aligned((x + 4 - dx) % 4, XCOLS), XCOLS)]
            src = rb.at[pl.ds(0, LOC), :]
            remote(src, dst, o_send.at[s, dx], o_recv.at[s, dx], z_dev).wait_recv()


def local(spatial_q, spatial_k, spatial_v, norm_gain, temporal_weight):
    dma = pltpu.SemaphoreType.DMA
    flat = [a.reshape(TOK, D) for a in (spatial_q, spatial_k, spatial_v)]
    hbm = pl.BlockSpec(memory_space=pl.ANY)
    out = pl.pallas_call(
        kernel,
        out_shape=jax.ShapeDtypeStruct((TOK, D), BF16),
        in_specs=[hbm, hbm, hbm, pl.BlockSpec(memory_space=pltpu.VMEM), hbm],
        out_specs=hbm,
        scratch_shapes=[
            pltpu.VMEM((HALF_TOK, XCOLS), BF16),
            pltpu.VMEM((HALF_TOK, XCOLS), BF16),
            pltpu.VMEM((HALF_TOK, XCOLS), BF16),
            pltpu.VMEM((2, 64, XCOLS), BF16),
            pltpu.VMEM((XHEADS, HALF_TOK, 128), F32),
            pltpu.VMEM((XHEADS, 128, HALF_TOK), BF16),
            pltpu.VMEM((2, XHEADS, 128, HEAD), BF16),
            pltpu.VMEM((2, 16, 128), F32),
            pltpu.VMEM((HALF_TOK, XCOLS), BF16),
            pltpu.VMEM((3, D, NCOLS), BF16),
            pltpu.VMEM((D, 3 * NCOLS), BF16),
            pltpu.VMEM((2, 4, HALF_TOK, XCOLS), BF16),
            pltpu.VMEM((3 * NHEADS, 2, 2, 16, LOC, HEAD), F32),
            pltpu.VMEM((2, 2, 16, LOC, 128), F32),
            pltpu.VMEM((2, 2, 16, LOC, NCOLS), BF16),
            pltpu.VMEM((HALF_TOK, XCOLS), BF16),
            dma((4, 4)), dma((4, 4)), dma((4,)),
            dma((4,)), dma((4,)),
            dma, dma((6,)), dma((6,)), dma((6,)), dma((6, 4)), dma((6, 4)),
            dma((32,)), dma((32,)), dma,
            dma((8, 4)), dma((8, 4)),
            dma((8, 4)), dma((8, 4)),
            dma((2, 32)), dma((2, 32)), dma,
            dma((8, 4)), dma((8, 4)), dma,
        ],
        compiler_params=pltpu.CompilerParams(collective_id=0, has_side_effects=True, vmem_limit_bytes=56 << 20),
    )(*flat, norm_gain.reshape(D // 128, 128), temporal_weight.transpose(1, 0, 2))
    return out.reshape(1, TOK, D)


def solution(mesh):
    return jax.shard_map(
        local,
        mesh=mesh,
        in_specs=(
            P("frame", "row", None),
            P("frame", "row", None),
            P("frame", "row", None),
            P(),
            P(None, None, "row"),
        ),
        out_specs=P("frame", "row", None),
        check_vma=False,
    )
```

```python
import jax
import jax.numpy as jnp
from jax import lax
from jax.experimental import pallas as pl
from jax.experimental.pallas import tpu as pltpu
from jax.sharding import PartitionSpec as P

D = 3072
HEAD = 128
TOK = 128
XCOLS = D // 4
XHEADS = XCOLS // HEAD
HALF_TOK = 4 * TOK
LOC = 16
NCOLS = D // 8
NHEADS = NCOLS // HEAD
SCALE = HEAD ** (-0.5)
EPS = 1e-06
F32 = jnp.float32
BF16 = jnp.bfloat16
MESH = pl.DeviceIdType.MESH


def aligned(i, n):
    return pl.multiple_of(i * n, n)


def kernel(
    q_hbm, k_hbm, v_hbm, gain, w_hbm, out,
    qx, kx, vx, ag, tw, pb, nb, st, sb, wv, ws, xb, acc, ssq, ob, rb,
    a_send, a_recv, a_loc, z_send, z_recv, w_loc, w1_send, w1_recv, wi_send, w2_send, w2_recv,
    b_send, b_recv, b_loc, x_send, x_recv, s_send, s_recv, c_send, c_recv, c_loc, o_send, o_recv, o_loc,
):
    f = lax.axis_index("frame")
    r = lax.axis_index("row")
    zl, y, c = f // 8, (f // 2) % 4, f % 2
    x, zh = r // 2, r % 2

    def dev(zl_, y_, c_, x_, zh_):
        return ((zl_ * 4 + y_) * 2 + c_, x_ * 2 + zh_)

    def remote(src, dst, ss, rs, to):
        return pltpu.make_async_remote_copy(src, dst, ss, rs, device_id=to, device_id_type=MESH)

    z_dev = dev(zl, y, c, x, 1 - zh)
    sib = dev(zl, y, 1 - c, x, zh)
    owner = c == zh

    barrier = pltpu.get_barrier_semaphore()
    for dx in (1, 3, 2):
        pl.semaphore_signal(barrier, inc=1, device_id=dev(zl, y, c, (x + dx) % 4, zh), device_id_type=MESH)

    for d in range(63, 0, -1):
        to = dev((zl + d // 16) % 4, (y + (d // 4) % 4) % 4, (c + d % 2) % 2, x, (zh + (d // 2) % 2) % 2)
        pl.semaphore_signal(barrier, inc=1, device_id=to, device_id_type=MESH)

    half_cols = XCOLS // 2
    parts = ((q_hbm, qx, 0, XCOLS), (k_hbm, kx, 0, XCOLS), (v_hbm, vx, 0, half_cols), (v_hbm, vx, half_cols, half_cols))

    def a_from(t, xp):
        src, _, lo, n = parts[t]
        return src.at[:, pl.ds(pl.multiple_of(xp * XCOLS + lo, 128), n)]

    def a_to(t):
        _, dst, lo, n = parts[t]
        return dst.at[pl.ds(aligned(x, TOK), TOK), pl.ds(lo, n)]

    def a_copy(t, dx):
        xp = (x + dx) % 4
        return remote(a_from(t, xp), a_to(t), a_send.at[t, dx], a_recv.at[t, dx], dev(zl, y, c, xp, zh))

    def a_local(t):
        return pltpu.make_async_copy(a_from(t, x), a_to(t), a_loc.at[t])

    def a_wait(t):
        for dx in (1, 3, 2):
            a_copy(t, dx).wait_recv()
        a_local(t).wait()

    edge = jnp.logical_or(zl == 0, zl == 3)
    away = jnp.logical_not(owner)

    def piece(y_, p):
        return ws.at[pl.ds(pl.multiple_of(y_ * 768 + p * 128, 128), 128), :]

    def w1_copy(p):
        return remote(piece(y, p), piece(y, p), w1_send.at[p], w1_recv.at[p], dev(3 - zl, y, c, x, 1 - zh))

    def wi_copy(p):
        to = dev(1 + zl // 3, y, c, x, zh)
        return remote(piece(y, p), piece(y, p), wi_send.at[p], w1_recv.at[p], to)

    def w2_copy(p, dy):
        to = dev(zl, (y + dy) % 4, c, x, zh)
        return remote(piece(y, p), piece(y, p), w2_send.at[p, dy], w2_recv.at[p, dy], to)

    def w_forward(outer, inner):
        def some(pieces, behind):
            for p in pieces:
                w1_copy(p).wait_recv()
                if behind:
                    wi_copy(p).start()
                for dy in (1, 3, 2):
                    w2_copy(p, dy).start()

        if outer:

            @pl.when(jnp.logical_and(away, edge))
            def _():
                some(outer, True)

        if inner:

            @pl.when(jnp.logical_and(away, jnp.logical_not(edge)))
            def _():
                some(inner, False)

    def w_scale(first, last):
        @pl.loop(first, last)
        def _(i):
            kc = (y * 6 + i) % 24
            g = jnp.broadcast_to(gain[pl.ds(kc, 1), :], (128, 128)).T
            rows = pl.ds(aligned(kc, 128), 128)
            for i in range(3):
                for j in range(NHEADS):
                    scaled = wv[i, rows, j * HEAD : (j + 1) * HEAD].astype(F32) * g
                    ws[rows, i * NCOLS + j * HEAD : i * NCOLS + (j + 1) * HEAD] = scaled.astype(BF16)

    for t in range(4):
        a_local(t).start()

    @pl.when(owner)
    def _():
        load = pltpu.make_async_copy(w_hbm, wv, w_loc)
        load.start()
        load.wait()
        w_scale(0, 6)

    pl.semaphore_wait(barrier, 66)
    for t in range(4):
        for dx in (1, 3, 2):
            a_copy(t, dx).start()

    @pl.when(jnp.logical_and(owner, edge))
    def _():
        for p in range(6):
            w1_copy(p).start()

    @pl.when(owner)
    def _():
        w_scale(6, 24)

    w_forward((0, 1), ())
    a_wait(0)
    pool = (
        lax.broadcasted_iota(jnp.int32, (64, HALF_TOK), 1) // 8 == lax.broadcasted_iota(jnp.int32, (64, HALF_TOK), 0)
    ).astype(F32) * 0.125
    ag[zh] = jnp.dot(pool.astype(BF16), qx[...], preferred_element_type=F32).astype(BF16)
    ag_copy = remote(ag.at[zh], ag.at[zh], z_send.at[0], z_recv.at[0], z_dev)
    ag_copy.start()
    w_forward((2, 3), (0,))
    ag_copy.wait_recv()

    def nt(a, b):
        return lax.dot_general(a, b, (((1,), (1,)), ((), ())), preferred_element_type=F32)

    def head(h):
        return slice(h * HEAD, (h + 1) * HEAD)

    def agents(h):
        return ag[:, :, head(h)].reshape(2 * 64, HEAD)

    for h in range(XHEADS):
        s = nt(qx[:, head(h)], agents(h)) * SCALE
        e = jnp.exp(s - jnp.max(s, axis=1, keepdims=True))
        tw[h] = e * (1.0 / jnp.sum(e, axis=1, keepdims=True))
    w_forward((4,), (1, 2))

    a_wait(1)
    lane = lax.broadcasted_iota(jnp.int32, (128, 128), 1)
    stats = jnp.where(lane < 8, 0.0, 1.0)
    for h in range(XHEADS):
        s = nt(agents(h), kx[:, head(h)]) * SCALE
        m = jnp.max(s, axis=1, keepdims=True)
        e = jnp.exp(s - m)
        pb[h] = e.astype(BF16)
        stats = jnp.where(lane == h, m, stats)
        stats = jnp.where(lane == 8 + h, jnp.sum(e, axis=1, keepdims=True), stats)
    st[zh] = stats.T[0:16, :]
    st_copy = remote(st.at[zh], st.at[zh], z_send.at[1], z_recv.at[1], z_dev)
    st_copy.start()
    w_forward((5,), (3,))

    def nb_copy(i):
        half = nb.at[zh, 3 * i : 3 * i + 3]
        return remote(half, half, z_send.at[2 + i], z_recv.at[2 + i], z_dev)

    for i in range(2):
        a_wait(2 + i)
        for h in range(3 * i, 3 * i + 3):
            nb[zh, h] = jnp.dot(pb[h], vx[:, head(h)], preferred_element_type=F32).astype(BF16)
        nb_copy(i).start()
    w_forward((), (4, 5))
    st_copy.wait_recv()
    m0, m1 = st[0, 0:8, :], st[1, 0:8, :]
    l0, l1 = st[0, 8:16, :], st[1, 8:16, :]
    peak = jnp.maximum(m0, m1)
    e0, e1 = jnp.exp(m0 - peak), jnp.exp(m1 - peak)
    inv = 1.0 / (l0 * e0 + l1 * e1)
    s0, s1 = e0 * inv, e1 * inv

    for h in range(XHEADS):
        if h % 3 == 0:
            nb_copy(h // 3).wait_recv()
        t = tw[h]
        both = jnp.concatenate([(t * s0[h : h + 1, :]).astype(BF16), (t * s1[h : h + 1, :]).astype(BF16)], axis=1)
        sb[:, head(h)] = jnp.dot(
            both, nb[:, h].reshape(256, HEAD), preferred_element_type=F32
        ).astype(BF16)

    z = zh * 4 + zl
    me = z * 4 + y

    def nearest(step):
        return (step % 2) * ((step + 1) // 2) + (1 - step % 2) * ((8 - step // 2) % 8)

    def b_copy(n):
        z_, y_ = (z + nearest(n // 4)) % 8, (y + n % 4) % 4
        return remote(
            sb.at[pl.ds(aligned(y_ * 8 + z_, LOC), LOC), :],
            xb.at[c, x, pl.ds(aligned(me, LOC), LOC), :],
            b_send.at[n], b_recv.at[n], dev(z_ % 4, y_, c, x, z_ // 4),
        )

    def b_wait(n):
        z_, y_ = (z + 8 - nearest(n // 4)) % 8, (y + 4 - n % 4) % 4
        dst = xb.at[c, x, pl.ds(aligned(z_ * 4 + y_, LOC), LOC), :]
        remote(dst, dst, b_send.at[n], b_recv.at[n], z_dev).wait_recv()

    group = y * 8 + z
    own = pltpu.make_async_copy(
        sb.at[pl.ds(aligned(group, LOC), LOC), :], xb.at[c, x, pl.ds(aligned(me, LOC), LOC), :], b_loc
    )
    own.start()

    def b_start(first, last):
        @pl.loop(first, last)
        def _(n):
            b_copy(n).start()

    b_start(1, 20)

    left, right, far = (x + 3) % 4, (x + 1) % 4, (x + 2) % 4

    def block(half, col, s, lo=0, n=64):
        z_ = (z + 8 - nearest(s)) % 8
        return xb.at[half, col, pl.ds(pl.multiple_of(z_ * 64 + lo, 32), n), :]

    def x_own(s, i):
        b = block(c, x, s)
        return remote(b, b, x_send.at[s, i], x_recv.at[s, i], dev(zl, y, c, (right, left)[i], zh))

    def x_fwd(s, i):
        b = block(c, (left, right)[i], s, 32 * i, 32)
        return remote(b, b, x_send.at[s, 2 + i], x_recv.at[s, 2 + i], dev(zl, y, c, (right, left)[i], zh))

    def x_got(s, i):
        col = (left, right, far, far)[i]
        b = block(c, col, s, *((0, 64), (0, 64), (0, 32), (32, 32))[i])
        return remote(b, b, x_send.at[s, i], x_recv.at[s, i], z_dev)

    def to_sib(s, i):
        b = block(c, (x, left, right, far)[i], s)
        return remote(b, b, s_send.at[s, i], s_recv.at[s, i], sib)

    def from_sib(s, i):
        b = block(1 - c, (x, left, right, far)[i], s)
        return remote(b, b, s_send.at[s, i], s_recv.at[s, i], sib)

    def mm(half, col, first=False):
        rows_w = pl.ds(aligned(col, XCOLS), XCOLS)

        @pl.loop(0, 2)
        def _(i):
            src = xb[half, col, pl.ds(aligned(i, 256), 256), :]
            p = jnp.dot(src, ws[rows_w, :], preferred_element_type=F32)
            wide = src.astype(F32)
            sq = jnp.broadcast_to(jnp.sum(wide * wide, axis=1, keepdims=True), (256, 128)).reshape(16, LOC, 128)
            for j in range(3 * NHEADS):
                pj = p[:, head(j)].reshape(16, LOC, 128)
                if first:
                    acc[j, half, i] = pj
                else:
                    acc[j, half, i] += pj
            if first:
                ssq[half, i] = sq
            else:
                ssq[half, i] += sq

    def sides(s):
        for i in range(2):
            x_got(s, i).wait_recv()
            x_fwd(s, i).start()
            to_sib(s, 1 + i).start()

    def ends(s):
        x_got(s, 2).wait_recv()
        x_got(s, 3).wait_recv()
        to_sib(s, 3).start()

    for s in range(8):
        if s == 0:
            own.wait()
        for n in range(4 * s, 4 * s + 4):
            if n:
                b_wait(n)
        if s < 3:
            b_start(4 * s + 20, 4 * s + 24)
        x_own(s, 0).start()
        x_own(s, 1).start()
        to_sib(s, 0).start()
        if s >= 1:
            sides(s - 1)
        if s >= 2:
            ends(s - 2)

    @pl.when(away)
    def _():
        for p in range(6):
            for dy in (1, 3, 2):
                dst = piece((y + 4 - dy) % 4, p)
                remote(dst, dst, w2_send.at[p, dy], w2_recv.at[p, dy], z_dev).wait_recv()

    mm(c, x, True)
    for s in range(8):
        from_sib(s, 0).wait_recv()
    mm(1 - c, x, True)
    sides(7)
    ends(6)
    mm(c, left)
    mm(c, right)
    for s in range(8):
        from_sib(s, 1).wait_recv()
        from_sib(s, 2).wait_recv()
    mm(1 - c, left)
    ends(7)
    mm(1 - c, right)
    mm(c, far)
    for s in range(8):
        from_sib(s, 3).wait_recv()
    mm(1 - c, far)
    ssq[...] = lax.rsqrt(ssq[...] * (1.0 / D) + EPS)

    same = lax.broadcasted_iota(jnp.int32, (256, 256), 0) % 8 == lax.broadcasted_iota(jnp.int32, (256, 256), 1) % 8

    def attend(zh_, lo):
        norm = ssq[:, zh_, :, lo : lo + 8, :].reshape(256, 128)

        def rows_of(j):
            return (acc[j, :, zh_, :, lo : lo + 8, :].reshape(256, 128) * norm).astype(BF16)

        for h in range(NHEADS):
            s = nt(rows_of(h), rows_of(NHEADS + h)) * SCALE
            s = jnp.where(same, s, -1e30)
            e = jnp.exp(s - jnp.max(s, axis=1, keepdims=True))
            p = (e * (1.0 / jnp.sum(e, axis=1, keepdims=True))).astype(BF16)
            o = jnp.dot(p, rows_of(2 * NHEADS + h), preferred_element_type=F32)
            ob[:, zh_, :, lo : lo + 8, head(h)] = o.astype(BF16).reshape(2, 16, 8, HEAD)

    def c_to(g, c_):
        return rb.at[pl.ds(aligned(g, LOC), LOC), pl.ds(aligned(c_, NCOLS), NCOLS)]

    def c_copy(d, hs):
        zl_, y_, c_, zh_ = (zl + d // 8) % 4, (y + (d // 2) % 4) % 4, (c + d % 2) % 2, (zh + hs) % 2
        src = ob.at[c_, zh_, zl_ * 4 + y_]
        return remote(src, c_to(group, c), c_send.at[hs, d], c_recv.at[hs, d], dev(zl_, y_, c_, x, zh_))

    def c_own():
        return pltpu.make_async_copy(ob.at[c, zh, zl * 4 + y], c_to(group, c), c_loc)

    for hs in (1, 0):
        for lo in (0, 8):
            attend((zh + hs) % 2, lo)

        @pl.loop(1 - hs, 32)
        def _(d):
            c_copy(d, hs).start()

    c_own().start()

    def c_wait(z_, y_, dc):
        d = ((zl + 4 - z_ % 4) % 4) * 8 + ((y + 4 - y_) % 4) * 2 + dc
        hs = (zh + z_ // 4) % 2
        dst = c_to(y_ * 8 + z_, (c + dc) % 2)

        @pl.when(d + hs > 0)
        def _():
            remote(dst, dst, c_send.at[hs, d], c_recv.at[hs, d], z_dev).wait_recv()

        @pl.when(d + hs == 0)
        def _():
            c_own().wait()

    def o_copy(s, dx):
        z_, xp = (z + 8 - nearest(s)) % 8, (x + dx) % 4
        return remote(
            rb.at[pl.ds(aligned(xp * 8 + z_, LOC), LOC), :],
            out.at[pl.ds(aligned(z_, LOC), LOC), pl.ds(aligned(x, XCOLS), XCOLS)],
            o_send.at[s, dx], o_recv.at[s, dx], dev(zl, y, c, xp, zh),
        )

    @pl.loop(0, 8)
    def _(s):
        z_ = (z + 8 - nearest(s)) % 8
        for dx in (1, 3, 2, 0):
            for dc in range(2):
                c_wait(z_, (x + dx) % 4, dc)
            if dx:
                o_copy(s, dx).start()

    mine = pltpu.make_async_copy(
        rb.at[pl.ds(aligned(x, TOK), TOK), :], out.at[:, pl.ds(aligned(x, XCOLS), XCOLS)], o_loc
    )
    mine.start()

    for t in range(4):
        for dx in (1, 3, 2):
            a_copy(t, dx).wait_send()

    @pl.when(jnp.logical_and(owner, edge))
    def _():
        for p in range(6):
            w1_copy(p).wait_send()

    @pl.when(jnp.logical_and(away, edge))
    def _():
        for p in range(6):
            wi_copy(p).wait_send()

    @pl.when(away)
    def _():
        for p in range(6):
            for dy in (1, 3, 2):
                w2_copy(p, dy).wait_send()

    ag_copy.wait_send()
    st_copy.wait_send()
    for i in range(2):
        nb_copy(i).wait_send()

    @pl.loop(1, 32)
    def _(d):
        b_copy(d).wait_send()

    for s in range(8):
        for i in range(2):
            x_own(s, i).wait_send()
            x_fwd(s, i).wait_send()
        for i in range(4):
            to_sib(s, i).wait_send()

    @pl.loop(1, 64)
    def _(d):
        c_copy(d % 32, d // 32).wait_send()

    mine.wait()

    @pl.loop(0, 8)
    def _(s):
        for dx in (1, 3, 2):
            o_copy(s, dx).wait_send()

    @pl.loop(0, 8)
    def _(s):
        z_ = (z + 8 - nearest(s)) % 8
        for dx in (1, 3, 2):
            dst = out.at[pl.ds(aligned(z_, LOC), LOC), pl.ds(aligned((x + 4 - dx) % 4, XCOLS), XCOLS)]
            src = rb.at[pl.ds(0, LOC), :]
            remote(src, dst, o_send.at[s, dx], o_recv.at[s, dx], z_dev).wait_recv()


def local(spatial_q, spatial_k, spatial_v, norm_gain, temporal_weight):
    dma = pltpu.SemaphoreType.DMA
    flat = [a.reshape(TOK, D) for a in (spatial_q, spatial_k, spatial_v)]
    hbm = pl.BlockSpec(memory_space=pl.ANY)
    out = pl.pallas_call(
        kernel,
        out_shape=jax.ShapeDtypeStruct((TOK, D), BF16),
        in_specs=[hbm, hbm, hbm, pl.BlockSpec(memory_space=pltpu.VMEM), hbm],
        out_specs=hbm,
        scratch_shapes=[
            pltpu.VMEM((HALF_TOK, XCOLS), BF16),
            pltpu.VMEM((HALF_TOK, XCOLS), BF16),
            pltpu.VMEM((HALF_TOK, XCOLS), BF16),
            pltpu.VMEM((2, 64, XCOLS), BF16),
            pltpu.VMEM((XHEADS, HALF_TOK, 128), F32),
            pltpu.VMEM((XHEADS, 128, HALF_TOK), BF16),
            pltpu.VMEM((2, XHEADS, 128, HEAD), BF16),
            pltpu.VMEM((2, 16, 128), F32),
            pltpu.VMEM((HALF_TOK, XCOLS), BF16),
            pltpu.VMEM((3, D, NCOLS), BF16),
            pltpu.VMEM((D, 3 * NCOLS), BF16),
            pltpu.VMEM((2, 4, HALF_TOK, XCOLS), BF16),
            pltpu.VMEM((3 * NHEADS, 2, 2, 16, LOC, HEAD), F32),
            pltpu.VMEM((2, 2, 16, LOC, 128), F32),
            pltpu.VMEM((2, 2, 16, LOC, NCOLS), BF16),
            pltpu.VMEM((HALF_TOK, XCOLS), BF16),
            dma((4, 4)), dma((4, 4)), dma((4,)),
            dma((4,)), dma((4,)),
            dma, dma((6,)), dma((6,)), dma((6,)), dma((6, 4)), dma((6, 4)),
            dma((32,)), dma((32,)), dma,
            dma((8, 4)), dma((8, 4)),
            dma((8, 4)), dma((8, 4)),
            dma((2, 32)), dma((2, 32)), dma,
            dma((8, 4)), dma((8, 4)), dma,
        ],
        compiler_params=pltpu.CompilerParams(collective_id=0, has_side_effects=True, vmem_limit_bytes=56 << 20),
    )(*flat, norm_gain.reshape(D // 128, 128), temporal_weight.transpose(1, 0, 2))
    return out.reshape(1, TOK, D)


def solution(mesh):
    return jax.shard_map(
        local,
        mesh=mesh,
        in_specs=(
            P("frame", "row", None),
            P("frame", "row", None),
            P("frame", "row", None),
            P(),
            P(None, None, "row"),
        ),
        out_specs=P("frame", "row", None),
        check_vma=False,
    )
```
